32 devices in a mesh: rep: 2 (over x), node: 2 (over core), local: 8 (over z, y).
Axes of the slice: x: 2, y: 2, z: 4, core: 2. Of those that a mesh axis runs over, the one named last changes fastest.
Arguments:
- attn_out: bfloat16 [64, 1024], P(('rep', 'node'), 'local'), parts along dimension 0, may hold values from -6 to 6
- o_proj: bfloat16 [1024, 7168], P('local'), may hold values from -0.1875 to 0.1875
- resid: bfloat16 [64, 7168], P(('rep', 'node', 'local')), parts along dimension 0, may hold values from -6 to 6
- norm_gain: float32 [7168], replicated, may hold values from 0.5 to 1.5
- routes: int32 [64, 8], P(('rep', 'node', 'local')), parts along dimension 0, may hold values from 0 to 15, all different within a row; in each aligned block of 2 rows (0 to 1, 2 to 3, ...) at most 2 rows name the same one
- route_w: bfloat16 [64, 8], P(('rep', 'node', 'local')), parts along dimension 0, may hold values from 0.19921875 to 1
- w_gate: bfloat16 [16, 7168, 2048], P(('node', 'local')), may hold values from -0.0625 to 0.0625
- w_up: bfloat16 [16, 7168, 2048], P(('node', 'local')), may hold values from -0.0625 to 0.0625
- w_down: bfloat16 [16, 2048, 7168], P(('node', 'local')), may hold values from -0.125 to 0.125
Outputs:
- layer_out: bfloat16 [64, 7168], P(('rep', 'node', 'local')), parts along dimension 0
The draws below stay inside these ranges and needn't reach their ends.
There are 2 independent parts, one for each index of `rep`. The reference program is written for one: setup_inputs(seed, part) draws one part's arguments, and reference() takes and returns one part's arrays. A program takes and returns all parts, laid end to end along the dimension named above; an argument that names none is the same for every part. Nothing has to cross between parts.
Inputs may be any that keep to these rules, and one draw needn't show every extreme that they name: `routes`: each row names 8 different experts. Within the rows of one device (aligned blocks of 2 rows) no expert is named more than 2 times, and in some block some expert is named exactly 2 times.
All inputs are finite; a program needn't handle non-finite values.
Results may differ from the reference program's by a relative error of at most 0.0075.
Values may be sent and summed in bfloat16 or wider, within the bound.
A program may use at most 128 MiB of HBM per device.

```python
import math
import jax
import jax.numpy as jnp
import numpy as np
from jax import lax

D = 7168
FF = 2048
HD = 128
GROUP_EXPERTS = 8
TOPK = 8
TOK_DEV = 2
MOST = 2
SHARDS = 1
F_DEV = 2048
EXPERTS = 16
HEADS = 8
TOKENS = 32
N_NODE = 2
N_LOCAL = 8


def spiked(drawn, own_key, source, target, shards_of, factor):
    owner, partner = [(jnp.arange(drawn.shape[dim]) // (drawn.shape[dim] // shards_of)).reshape([-1 if axis == dim else 1 for axis in range(drawn.ndim)]) for dim in (source, target)]
    chosen = jax.random.permutation(own_key, shards_of)[partner]
    strong = (owner == chosen) | (owner == (partner + shards_of // 2) % shards_of)
    return jnp.where(strong, factor * drawn, drawn)


def levels(stream_key, extent, split, smallest, largest):
    factor_of = 1.0
    for dim, shards_of in split:
        steps = jax.random.uniform(jax.random.fold_in(jax.random.fold_in(stream_key, 6), dim), (shards_of,), jnp.float32, smallest / len(split), largest / len(split))
        factor_of = factor_of * jnp.repeat(jnp.exp(steps), extent[dim] // shards_of).reshape((-1,) + (1,) * (len(extent) - 1 - dim))
    return factor_of


def assign_block(own_key, own, number, rows, count, top, reach, lean):
    ranking = jax.random.permutation(own_key, count)
    packed, common = portions_of(count, rows * top, reach, lean, True), portions_of(count, rows * top, reach, lean, False)
    places = jnp.arange(count)

    def named(lengths, rotation):
        used = int((lengths > 0).sum())
        fixed = max(1, used // 4)
        moved = fixed + (places - fixed + rotation * (used - fixed)) % max(1, count - fixed)
        return jnp.zeros((count,), jnp.int32).at[ranking[jnp.where(places < fixed, places, moved)]].set(jnp.asarray(lengths, jnp.int32))

    lengths = jnp.where(number % 4 == 0, named(packed, number // 4), named(common, number - number // 4 - 1))
    mixed = jax.random.permutation(jax.random.fold_in(own, 3), count)
    donor, sink = mixed[0:count // 2 * 2:2], mixed[1:count // 2 * 2:2]
    margin = jnp.minimum(lengths[donor] - 1, reach - lengths[sink]) // 2
    margin = jnp.where((donor == ranking[0]) | (sink == ranking[0]) | (lengths[sink] == 0), 0, jnp.maximum(margin, 0))
    moved = jax.random.randint(jax.random.fold_in(own, 4), (count // 2,), 0, 1 << 20) % (margin + 1)
    lengths = lengths.at[donor].add(-moved).at[sink].add(moved)
    members = jnp.searchsorted(jnp.cumsum(lengths), jnp.arange(rows * top), side="right").astype(jnp.int32)
    table = members.reshape(top, rows).T
    table = table[jax.random.permutation(jax.random.fold_in(own, 1), rows)]
    rotation = jax.random.randint(jax.random.fold_in(own, 2), (rows, 1), 0, top)
    return jnp.take_along_axis(table, (jnp.arange(top)[None, :] + rotation) % top, axis=1)


def portions_of(amount, total, reach, slope, full):
    portions = [(1 << 20) // math.isqrt(grade ** slope) + 1 for grade in range(1, amount + 1)]
    largest = reach if full else min(reach, max(-(-total // amount), total * portions[0] // sum(portions)))
    least = 1 if total - largest >= amount - 1 else 0
    counts, rest = [largest] + [least] * (amount - 1), total - largest - least * (amount - 1)
    while rest > 0:
        movable = [i for i in range(1, amount) if counts[i] < largest] or [i for i in range(1, amount) if counts[i] < reach]
        pool, remaining = sum([portions[i] for i in movable]), rest
        for i in movable:
            more = min(reach - counts[i], max(1, remaining * portions[i] // pool), rest)
            counts[i] = counts[i] + more
            rest = rest - more
    return np.array(counts)


def normal_values(own_key, extent, spread, limit, cuts=(), held_as=jnp.bfloat16):
    drawn = spread * jax.random.normal(own_key, extent, jnp.float32)
    if cuts:
        drawn = drawn * levels(own_key, extent, cuts, -0.22, 0.18)
    return jnp.clip(drawn, -limit, limit).astype(held_as)


def noise_with(own_key, shape, scale, bound, cuts, heavy, kind=jnp.bfloat16):
    values = scale * jax.random.normal(own_key, shape, jnp.float32)
    if cuts:
        values = values * levels(own_key, shape, cuts, -0.22, 0.18)
    return jnp.clip(spiked(values, jax.random.fold_in(own_key, 3), *heavy), -bound, bound).astype(kind)


def setup_inputs(seed: int = 0, part: int = 0) -> dict:
    streams_of = jax.random.split(jax.random.key(seed), 10)
    part_keys = jax.random.split(jax.random.fold_in(streams_of[9], part), 10)
    attn_out = noise_with(part_keys[0], (TOKENS, HEADS * HD), 1.0, 6.0, ((0, 2), (1, 8)), (1, 0, 8, 2.0))
    o_proj = normal_values(streams_of[1], (HEADS * HD, D), (HEADS * HD) ** -0.5, 0.1875, ((0, 8),))
    resid = normal_values(part_keys[2], (TOKENS, D), 1.0, 6.0, ((0, 16),))
    norm_gain = jnp.clip(1.0 + 0.1 * jax.random.normal(streams_of[3], (D,), jnp.float32), 0.5, 1.5)
    routes_keys = jax.random.split(jax.random.fold_in(part_keys[4], 1), TOKENS // TOK_DEV)
    routes_turns = jax.random.permutation(jax.random.fold_in(part_keys[4], 3), TOKENS // TOK_DEV)
    routes = jax.vmap(lambda own, number: assign_block(jax.random.fold_in(part_keys[4], 2), own, number, TOK_DEV, EXPERTS, TOPK, MOST, 2))(routes_keys, routes_turns).reshape((TOKENS, TOPK))
    route_w = jnp.clip(0.19921875 + 0.80078125 * jax.random.uniform(part_keys[5], (TOKENS, TOPK), jnp.float32) ** levels(part_keys[5], (TOKENS, TOPK), ((0, 16),), -0.2, 0.2), 0.19921875, 1.0).astype(jnp.bfloat16)
    w_gate = normal_values(streams_of[6], (EXPERTS * SHARDS, D, F_DEV), D ** -0.5, 0.0625, ((0, 16),))
    w_up = normal_values(streams_of[7], (EXPERTS * SHARDS, D, F_DEV), D ** -0.5, 0.0625, ((0, 16),))
    w_down = normal_values(streams_of[8], (EXPERTS * SHARDS, F_DEV, D), FF ** -0.5, 0.125, ((0, 16),))
    return dict(attn_out=attn_out, o_proj=o_proj, resid=resid, norm_gain=norm_gain, routes=routes, route_w=route_w, w_gate=w_gate, w_up=w_up, w_down=w_down)


def reference(attn_out, o_proj, resid, norm_gain, routes, route_w, w_gate, w_up, w_down):
    projected = jnp.dot(attn_out, o_proj, preferred_element_type=jnp.float32)
    hidden = resid.astype(jnp.float32) + projected
    mean_sq = lax.optimization_barrier(jnp.mean(hidden * hidden, axis=-1, keepdims=True))
    normed = (hidden * lax.rsqrt(mean_sq + 1e-06) * norm_gain.astype(jnp.float32)).astype(jnp.bfloat16)
    flat_ids = routes.reshape(-1).astype(jnp.int32)
    flat_weights = route_w.reshape(-1).astype(jnp.float32)
    token_of = (jnp.arange(TOKENS * TOPK) // TOPK).astype(jnp.int32)
    row_cap = min(TOKENS, N_NODE * N_LOCAL * MOST)
    model_width = o_proj.shape[1]
    hidden_dev = w_gate.shape[2]
    group_count = EXPERTS // GROUP_EXPERTS

    def one_expert(groups, expert):
        picked = jnp.argsort((flat_ids != expert).astype(jnp.int32), stable=True)[:row_cap].astype(jnp.int32)
        usable = flat_ids[picked] == expert
        tokens = token_of[picked]
        chosen_rows = normed[tokens]
        first_row = (expert * SHARDS).astype(jnp.int32)
        gate_w = lax.dynamic_slice_in_dim(w_gate, first_row, SHARDS, 0)
        up_w = lax.dynamic_slice_in_dim(w_up, first_row, SHARDS, 0)
        down_w = lax.dynamic_slice_in_dim(w_down, first_row, SHARDS, 0)
        gate_joined = jnp.transpose(gate_w, (1, 0, 2)).reshape(model_width, SHARDS * hidden_dev)
        up_joined = jnp.transpose(up_w, (1, 0, 2)).reshape(model_width, SHARDS * hidden_dev)
        gate_val = jnp.dot(chosen_rows, gate_joined, preferred_element_type=jnp.float32)
        up_val = jnp.dot(chosen_rows, up_joined, preferred_element_type=jnp.float32)
        activated = (jax.nn.silu(gate_val) * up_val).astype(jnp.bfloat16).reshape(row_cap, SHARDS, hidden_dev)
        pieces = jnp.einsum('rsf,sfd->rsd', activated.astype(jnp.float32), down_w.astype(jnp.float32)).astype(jnp.bfloat16)
        expert_out = lax.optimization_barrier(jnp.sum(pieces.astype(jnp.float32), axis=1))
        coeffs = jnp.where(usable, flat_weights[picked], jnp.zeros_like(flat_weights[picked]))
        group_idx = expert // GROUP_EXPERTS
        groups = groups.at[group_idx, tokens].add(coeffs[:, None] * expert_out)
        return (groups, None)
    initial = jnp.zeros((group_count, TOKENS, model_width), jnp.float32)
    groups, _ = lax.scan(one_expert, initial, jnp.arange(EXPERTS, dtype=jnp.int32))
    rounded = groups.astype(jnp.bfloat16).astype(jnp.float32)
    summed = hidden
    for group_idx in range(group_count):
        summed = summed + rounded[group_idx]
    return summed.astype(jnp.bfloat16)
```

```python
import functools

import jax
import jax.numpy as jnp
from jax import lax
from jax.experimental import pallas as pl
from jax.experimental.pallas import tpu as pltpu
from jax.sharding import PartitionSpec as P

GROUP_EXPERTS = 8
MESH = pl.DeviceIdType.MESH


def layer_kernel(
    nodes,
    locals_,
    attn_ref,
    oproj_hbm,
    resid_ref,
    gain_ref,
    routes_ref,
    weight_ref,
    gate_hbm,
    up_hbm,
    down_hbm,
    out_ref,
    oproj,
    slots,
    part_out,
    part_in,
    hidden,
    gathered,
    rows,
    gate_acc,
    up_acc,
    act,
    piece_out,
    piece_in,
    oproj_sem,
    slot_sem,
    part_send,
    part_recv,
    gather_send,
    gather_recv,
    relay_send,
    piece_send,
    piece_recv,
):
    node = lax.axis_index("node")
    local = lax.axis_index("local")
    members = nodes * locals_
    me = node * locals_ + local
    chunk, hidden_units = slots.shape[1], slots.shape[2]
    blocks = hidden_units // chunk
    toks, width = resid_ref.shape
    pairs = width // chunk

    def device(member):
        return {"node": lax.div(member, locals_), "local": lax.rem(member, locals_)}

    def up_copies(i):
        start = pl.ds(pl.multiple_of(i * chunk, chunk), chunk)
        return (
            pltpu.make_async_copy(gate_hbm.at[0, start], slots.at[2 * i], slot_sem.at[2 * i, 0]),
            pltpu.make_async_copy(up_hbm.at[0, start], slots.at[2 * i + 1], slot_sem.at[2 * i + 1, 0]),
        )

    def down_copies(j):
        cols = pl.ds(pl.multiple_of(j * chunk, chunk), chunk)
        return [
            pltpu.make_async_copy(
                down_hbm.at[0, pl.ds(b * chunk, chunk), cols],
                slots.at[j, :, pl.ds(b * chunk, chunk)],
                slot_sem.at[j, b],
            )
            for b in range(blocks)
        ]

    load_oproj = pltpu.make_async_copy(oproj_hbm, oproj, oproj_sem)
    load_oproj.start()

    barrier = pltpu.get_barrier_semaphore()

    def greet(off, carry):
        pl.semaphore_signal(
            barrier, inc=1, device_id=device(lax.rem(me + off, members)), device_id_type=MESH
        )
        return carry

    lax.fori_loop(1, members, greet, 0)

    def fill(i, carry):
        for copy in up_copies(i):
            copy.start()
        return carry

    lax.fori_loop(0, pairs, fill, 0)

    load_oproj.wait()
    for j in range(width // chunk):
        cols = slice(j * chunk, (j + 1) * chunk)
        partial = jnp.dot(attn_ref[...], oproj[:, cols], preferred_element_type=jnp.float32)
        for peer in range(locals_):
            part_out[peer, :, cols] = partial[peer * toks : (peer + 1) * toks].astype(jnp.bfloat16)
    pl.semaphore_wait(barrier, members - 1)

    def part_copy(peer, slot):
        return pltpu.make_async_remote_copy(
            src_ref=part_out.at[peer],
            dst_ref=part_in.at[slot],
            send_sem=part_send.at[peer],
            recv_sem=part_recv.at[slot],
            device_id={"local": peer},
            device_id_type=MESH,
        )

    def send_part(off, carry):
        part_copy(lax.rem(local + off, locals_), local).start()
        return carry

    lax.fori_loop(1, locals_, send_part, 0)
    hidden[...] = resid_ref[...].astype(jnp.float32) + part_out[local].astype(jnp.float32)

    def take_part(off, carry):
        peer = lax.rem(local + off, locals_)
        part_copy(peer, peer).wait_recv()
        hidden[...] += part_in[peer].astype(jnp.float32)
        return carry

    lax.fori_loop(1, locals_, take_part, 0)
    value = hidden[...]
    mean_sq = jnp.mean(value * value, axis=-1, keepdims=True)
    gathered[me] = (value * lax.rsqrt(mean_sq + 1e-06) * gain_ref[...]).astype(jnp.bfloat16)

    def gather_copy(peer, slot):
        return pltpu.make_async_remote_copy(
            src_ref=gathered.at[slot],
            dst_ref=gathered.at[slot],
            send_sem=gather_send.at[peer],
            recv_sem=gather_recv.at[slot],
            device_id={"local": peer},
            device_id_type=MESH,
        )

    def relay_copy(off, slot):
        return pltpu.make_async_remote_copy(
            src_ref=gathered.at[slot],
            dst_ref=gathered.at[slot],
            send_sem=relay_send.at[off, slot],
            recv_sem=gather_recv.at[slot],
            device_id={"node": lax.rem(node + off, nodes)},
            device_id_type=MESH,
        )

    def send_token(off, carry):
        gather_copy(lax.rem(local + off, locals_), me).start()
        return carry

    lax.fori_loop(1, locals_, send_token, 0)
    for off in range(1, nodes):
        relay_copy(off, me).start()

    def take_token(dist, carry):
        peer = lax.rem(local + dist, locals_)
        slot = node * locals_ + peer
        gather_copy(peer, slot).wait_recv()
        for off in range(1, nodes):
            relay_copy(off, slot).start()
        return carry

    lax.fori_loop(1, locals_, take_token, 0)

    def take_relayed(dist, carry):
        peer = lax.rem(local + dist, locals_)
        for off in range(1, nodes):
            relay_copy(off, lax.rem(node + off, nodes) * locals_ + peer).wait_recv()
        return carry

    lax.fori_loop(0, locals_, take_relayed, 0)
    for member in range(members):
        rows[member * toks : (member + 1) * toks, :] = gathered[member]

    gate_acc[...] = jnp.zeros_like(gate_acc)
    up_acc[...] = jnp.zeros_like(up_acc)

    def project_up(i, carry):
        for copy in up_copies(i):
            copy.wait()
        lhs = rows[:, pl.ds(pl.multiple_of(i * chunk, chunk), chunk)]
        gate_acc[...] += jnp.dot(lhs, slots[2 * i], preferred_element_type=jnp.float32)
        up_acc[...] += jnp.dot(lhs, slots[2 * i + 1], preferred_element_type=jnp.float32)
        for late in range(2):
            @pl.when(2 * i + late < pairs)
            def _():
                for copy in down_copies(2 * i + late):
                    copy.start()
        return carry

    lax.fori_loop(0, pairs, project_up, 0)
    gate_val = gate_acc[...]
    act[...] = (gate_val / (1.0 + jnp.exp(-gate_val)) * up_acc[...]).astype(jnp.bfloat16)

    def piece_copy(peer, slot, cols):
        return pltpu.make_async_remote_copy(
            src_ref=piece_out.at[peer, :, cols],
            dst_ref=piece_in.at[slot, :, cols],
            send_sem=piece_send.at[peer],
            recv_sem=piece_recv.at[slot],
            device_id=device(peer),
            device_id_type=MESH,
        )

    def project_down(j, carry):
        for copy in down_copies(j):
            copy.wait()
        cols = pl.ds(pl.multiple_of(j * chunk, chunk), chunk)
        total = jnp.dot(act[:, :chunk], slots[j, :, :chunk], preferred_element_type=jnp.float32)
        for b in range(1, blocks):
            span = slice(b * chunk, (b + 1) * chunk)
            total += jnp.dot(act[:, span], slots[j, :, span], preferred_element_type=jnp.float32)
        for peer in range(members):
            piece_out[peer, :, cols] = total[peer * toks : (peer + 1) * toks].astype(jnp.bfloat16)

        def send_piece(off, inner):
            piece_copy(lax.rem(me + off, members), me, cols).start()
            return inner

        lax.fori_loop(1, members, send_piece, 0)
        return carry

    lax.fori_loop(0, pairs, project_down, 0)
    piece_in[me] = piece_out[me]

    every = pl.ds(0, width)

    def take_piece(off, carry):
        peer = lax.rem(me + off, members)
        piece_copy(peer, peer, every).wait_recv()
        return carry

    shard_count = locals_ // GROUP_EXPERTS
    span = members * toks
    depth = max(8, nodes * toks)
    repeats = depth // toks
    shape = (depth, span)
    row = lax.broadcasted_iota(jnp.int32, shape, 0).astype(jnp.float32)
    col = lax.broadcasted_iota(jnp.int32, shape, 1).astype(jnp.float32)
    row_group = jnp.floor((row + 0.5) * (1.0 / toks))
    row_tok = row - toks * row_group
    col_member = jnp.floor((col + 0.5) * (1.0 / toks))
    col_tok = col - toks * col_member
    col_expert = jnp.floor((col_member + 0.5) * (1.0 / shard_count))
    col_group = jnp.floor((col_expert + 0.5) * (1.0 / GROUP_EXPERTS))
    picks = jnp.concatenate([routes_ref[...].astype(jnp.float32)] * repeats, axis=0)
    scales = jnp.concatenate([weight_ref[...].astype(jnp.float32)] * repeats, axis=0)
    mixing = jnp.zeros(shape, jnp.float32)
    for k in range(picks.shape[1]):
        mixing += jnp.where(picks[:, k : k + 1] == col_expert, scales[:, k : k + 1], 0.0)
    mixing = jnp.where((row_tok == col_tok) & (row_group == col_group), mixing, 0.0).astype(jnp.bfloat16)

    lax.fori_loop(1, members, take_piece, 0)
    for member in range(members):
        rows[member * toks : (member + 1) * toks, :] = piece_in[member]
    for j in range(pairs):
        cols = slice(j * chunk, (j + 1) * chunk)
        mixed = jnp.dot(mixing, rows[:, cols], preferred_element_type=jnp.float32)
        summed = hidden[:, cols]
        for group in range(nodes):
            group_out = mixed[group * toks : (group + 1) * toks].astype(jnp.bfloat16)
            summed = summed + group_out.astype(jnp.float32)
        out_ref[:, cols] = summed.astype(jnp.bfloat16)

    def drain_local(off, carry):
        peer = lax.rem(local + off, locals_)
        part_copy(peer, local).wait_send()
        gather_copy(peer, me).wait_send()
        return carry

    lax.fori_loop(1, locals_, drain_local, 0)

    def drain_relay(peer, carry):
        for off in range(1, nodes):
            relay_copy(off, node * locals_ + peer).wait_send()
        return carry

    lax.fori_loop(0, locals_, drain_relay, 0)

    def drain_piece(off, carry):
        piece_copy(lax.rem(me + off, members), me, every).wait_send()
        return carry

    lax.fori_loop(1, members, drain_piece, 0)


def solution(mesh):
    nodes, locals_ = mesh.shape["node"], mesh.shape["local"]
    members = nodes * locals_

    def shards(attn_out, o_proj, resid, norm_gain, routes, route_w, w_gate, w_up, w_down):
        toks, width = resid.shape
        hidden_units = w_gate.shape[2]
        chunk = next(c for c in (512, 256, 128) if hidden_units % c == 0 and width % c == 0)
        pairs = width // chunk
        blocks = hidden_units // chunk
        bf16, f32 = jnp.bfloat16, jnp.float32
        vmem = pl.BlockSpec(memory_space=pltpu.VMEM)
        hbm = pl.BlockSpec(memory_space=pl.ANY)
        dma = pltpu.SemaphoreType.DMA
        total = members * toks
        return pl.pallas_call(
            functools.partial(layer_kernel, nodes, locals_),
            out_shape=jax.ShapeDtypeStruct((toks, width), bf16),
            in_specs=[vmem, hbm, vmem, vmem, vmem, vmem, hbm, hbm, hbm],
            out_specs=vmem,
            scratch_shapes=[
                pltpu.VMEM(o_proj.shape, bf16),
                pltpu.VMEM((2 * pairs, chunk, hidden_units), bf16),
                pltpu.VMEM((locals_, toks, width), bf16),
                pltpu.VMEM((locals_, toks, width), bf16),
                pltpu.VMEM((toks, width), f32),
                pltpu.VMEM((members, toks, width), bf16),
                pltpu.VMEM((total, width), bf16),
                pltpu.VMEM((total, hidden_units), f32),
                pltpu.VMEM((total, hidden_units), f32),
                pltpu.VMEM((total, hidden_units), bf16),
                pltpu.VMEM((members, toks, width), bf16),
                pltpu.VMEM((members, toks, width), bf16),
                dma,
                dma((2 * pairs, blocks)),
                dma((locals_,)),
                dma((locals_,)),
                dma((locals_,)),
                dma((members,)),
                dma((nodes, members)),
                dma((members,)),
                dma((members,)),
            ],
            compiler_params=pltpu.CompilerParams(
                collective_id=0, has_side_effects=True, vmem_limit_bytes=67043328
            ),
            name="moe_layer",
        )(attn_out, o_proj, resid, norm_gain.reshape(1, width), routes, route_w, w_gate, w_up, w_down)

    placed = (
        P(("rep", "node"), "local"),
        P("local", None),
        P(("rep", "node", "local"), None),
        P(),
        P(("rep", "node", "local"), None),
        P(("rep", "node", "local"), None),
        P(("node", "local"), None, None),
        P(("node", "local"), None, None),
        P(("node", "local"), None, None),
    )
    return jax.shard_map(
        shards,
        mesh=mesh,
        in_specs=placed,
        out_specs=P(("rep", "node", "local"), None),
        check_vma=False,
    )
```

```python
import functools

import jax
import jax.numpy as jnp
from jax import lax
from jax.experimental import pallas as pl
from jax.experimental.pallas import tpu as pltpu
from jax.sharding import PartitionSpec as P

GROUP_EXPERTS = 8
MESH = pl.DeviceIdType.MESH


def layer_kernel(
    nodes,
    locals_,
    stages,
    attn_ref,
    oproj_hbm,
    resid_ref,
    gain_ref,
    routes_ref,
    weight_ref,
    gate_hbm,
    up_hbm,
    down_hbm,
    out_ref,
    oproj,
    slots,
    part_out,
    part_in,
    hidden,
    gathered,
    rows,
    meta,
    meta_rows,
    gate_acc,
    up_acc,
    act,
    weighted,
    cross_out,
    cross_in,
    piece_out,
    piece_in,
    oproj_sem,
    slot_sem,
    part_send,
    part_recv,
    gather_send,
    gather_recv,
    relay_send,
    meta_send,
    meta_recv,
    meta_relay_send,
    cross_send,
    cross_recv,
    piece_send,
    piece_recv,
):
    node = lax.axis_index("node")
    local = lax.axis_index("local")
    members = nodes * locals_
    me = node * locals_ + local
    chunk, hidden_units = slots.shape[1], slots.shape[2]
    blocks = hidden_units // chunk
    toks, width = resid_ref.shape
    pairs = width // chunk
    stage_width = width // stages
    stage_pairs = pairs // stages
    half = locals_ * toks
    every = pl.ds(0, width)

    def stage_cols(s):
        return every if s is None else pl.ds(s * stage_width, stage_width)

    def chunk_cols(j):
        return pl.ds(pl.multiple_of(j * chunk, chunk), chunk)

    def peer_loop(first, body):
        def step(dist, carry):
            body(lax.rem(local + dist, locals_))
            return carry

        lax.fori_loop(first, locals_, step, 0)

    def up_copies(i):
        return (
            pltpu.make_async_copy(gate_hbm.at[0, chunk_cols(i)], slots.at[2 * i], slot_sem.at[2 * i, 0]),
            pltpu.make_async_copy(up_hbm.at[0, chunk_cols(i)], slots.at[2 * i + 1], slot_sem.at[2 * i + 1, 0]),
        )

    def down_copies(j):
        return [
            pltpu.make_async_copy(
                down_hbm.at[0, pl.ds(b * chunk, chunk), chunk_cols(j)],
                slots.at[j, :, pl.ds(b * chunk, chunk)],
                slot_sem.at[j, b],
            )
            for b in range(blocks)
        ]

    load_oproj = pltpu.make_async_copy(oproj_hbm, oproj, oproj_sem)
    load_oproj.start()

    barrier = pltpu.get_barrier_semaphore()

    def greet(peer):
        pl.semaphore_signal(barrier, inc=1, device_id={"local": peer}, device_id_type=MESH)

    peer_loop(1, greet)
    for off in range(1, nodes):
        pl.semaphore_signal(
            barrier, inc=1, device_id={"node": lax.rem(node + off, nodes)}, device_id_type=MESH
        )

    def fill(i, carry):
        for copy in up_copies(i):
            copy.start()
        return carry

    lax.fori_loop(0, pairs, fill, 0)

    def part_copy(peer, slot, s):
        return pltpu.make_async_remote_copy(
            src_ref=part_out.at[peer, :, stage_cols(s)],
            dst_ref=part_in.at[slot, :, stage_cols(s)],
            send_sem=part_send.at[peer],
            recv_sem=part_recv.at[slot, s or 0],
            device_id={"local": peer},
            device_id_type=MESH,
        )

    def gather_copy(peer, slot, s):
        return pltpu.make_async_remote_copy(
            src_ref=gathered.at[slot, :, stage_cols(s)],
            dst_ref=gathered.at[slot, :, stage_cols(s)],
            send_sem=gather_send.at[peer],
            recv_sem=gather_recv.at[slot, s or 0],
            device_id={"local": peer},
            device_id_type=MESH,
        )

    def relay_copy(off, slot, s):
        return pltpu.make_async_remote_copy(
            src_ref=gathered.at[slot, :, stage_cols(s)],
            dst_ref=gathered.at[slot, :, stage_cols(s)],
            send_sem=relay_send.at[off - 1, lax.rem(slot, locals_)],
            recv_sem=gather_recv.at[slot, s or 0],
            device_id={"node": lax.rem(node + off, nodes)},
            device_id_type=MESH,
        )

    def meta_copy(peer, slot):
        return pltpu.make_async_remote_copy(
            src_ref=meta.at[slot],
            dst_ref=meta.at[slot],
            send_sem=meta_send.at[peer],
            recv_sem=meta_recv.at[slot],
            device_id={"local": peer},
            device_id_type=MESH,
        )

    def meta_relay(off, slot):
        return pltpu.make_async_remote_copy(
            src_ref=meta.at[slot],
            dst_ref=meta.at[slot],
            send_sem=meta_relay_send.at[off - 1, lax.rem(slot, locals_)],
            recv_sem=meta_recv.at[slot],
            device_id={"node": lax.rem(node + off, nodes)},
            device_id_type=MESH,
        )

    load_oproj.wait()
    for s in range(stages):
        cols = stage_cols(s)
        partial = jnp.dot(attn_ref[...], oproj[:, cols], preferred_element_type=jnp.float32)
        for peer in range(locals_):
            part_out[peer, :, cols] = partial[peer * toks : (peer + 1) * toks].astype(jnp.bfloat16)
        if s == 0:
            pl.semaphore_wait(barrier, locals_ - 1 + nodes - 1)
        peer_loop(1, lambda peer: part_copy(peer, local, s).start())

    gate_acc[...] = jnp.zeros_like(gate_acc)
    up_acc[...] = jnp.zeros_like(up_acc)

    def reduce_stage(s):
        cols = stage_cols(s)
        peer_loop(1, lambda peer: part_copy(peer, peer, s).wait_recv())
        part_in[local, :, cols] = part_out[local, :, cols]
        value = resid_ref[:, cols].astype(jnp.float32)
        for peer in range(locals_):
            value += part_in[peer, :, cols].astype(jnp.float32)
        hidden[:, cols] = value
        gathered[me, :, cols] = (value * gain_ref[:, cols]).astype(jnp.bfloat16)
        peer_loop(1, lambda peer: gather_copy(peer, me, s).start())
        for off in range(1, nodes):
            relay_copy(off, me, s).start()

    def send_meta():
        value = hidden[...]
        scale = lax.rsqrt(jnp.mean(value * value, axis=-1, keepdims=True) + 1e-06)
        lane = lax.broadcasted_iota(jnp.int32, (toks, 128), 1)
        picks, scales = routes_ref[...], weight_ref[...].astype(jnp.float32)
        shares = jnp.zeros((toks, 128), jnp.float32)
        for k in range(picks.shape[1]):
            shares += jnp.where(picks[:, k : k + 1] == lane, scales[:, k : k + 1], 0.0)
        meta[me] = jnp.where(lane == 127, scale, shares)
        peer_loop(1, lambda peer: meta_copy(peer, me).start())
        for off in range(1, nodes):
            meta_relay(off, me).start()

    def relay_stage(s):
        def forward(peer):
            slot = node * locals_ + peer
            gather_copy(peer, slot, s).wait_recv()
            for off in range(1, nodes):
                relay_copy(off, slot, s).start()

        peer_loop(1, forward)

    def project_up(i, carry):
        for copy in up_copies(i):
            copy.wait()
        lhs = rows[:, chunk_cols(i)]
        gate_acc[...] += jnp.dot(lhs, slots[2 * i], preferred_element_type=jnp.float32)
        up_acc[...] += jnp.dot(lhs, slots[2 * i + 1], preferred_element_type=jnp.float32)
        for late in range(2):

            @pl.when(2 * i + late < pairs)
            def _():
                for copy in down_copies(2 * i + late):
                    copy.start()

        return carry

    def multiply_stage(s):
        def arrive(peer):
            for off in range(1, nodes):
                relay_copy(off, lax.rem(node + off, nodes) * locals_ + peer, s).wait_recv()

        peer_loop(0, arrive)
        cols = stage_cols(s)
        for member in range(members):
            rows[member * toks : (member + 1) * toks, cols] = gathered[member, :, cols]
        lax.fori_loop(s * stage_pairs, (s + 1) * stage_pairs, project_up, 0)

    for step in range(stages + 2):
        if step < stages:
            reduce_stage(step)
        if step == stages - 1:
            send_meta()
        if 1 <= step <= stages:
            relay_stage(step - 1)
        if step == stages:

            def forward_meta(peer):
                slot = node * locals_ + peer
                meta_copy(peer, slot).wait_recv()
                for off in range(1, nodes):
                    meta_relay(off, slot).start()

            peer_loop(1, forward_meta)
        if step >= 2:
            multiply_stage(step - 2)

    def meta_arrive(peer):
        for off in range(1, nodes):
            meta_relay(off, lax.rem(node + off, nodes) * locals_ + peer).wait_recv()

    peer_loop(0, meta_arrive)
    for member in range(members):
        meta_rows[member * toks : (member + 1) * toks, :] = meta[member]
    facts = meta_rows[...]
    lane = lax.broadcasted_iota(jnp.int32, facts.shape, 1)
    expert = lax.div(me, locals_ // GROUP_EXPERTS)
    share = jnp.sum(jnp.where(lane == expert, facts, 0.0), axis=1, keepdims=True)
    scale = jnp.sum(jnp.where(lane == 127, facts, 0.0), axis=1, keepdims=True)
    for b in range(blocks):
        span = slice(b * chunk, (b + 1) * chunk)
        gate_val = gate_acc[:, span] * scale
        up_val = up_acc[:, span] * (scale * share)
        act[:, span] = (gate_val / (1.0 + jnp.exp(-gate_val)) * up_val).astype(jnp.bfloat16)

    def cross_copy(off, j):
        return pltpu.make_async_remote_copy(
            src_ref=cross_out.at[off - 1, j],
            dst_ref=cross_in.at[off - 1, j],
            send_sem=cross_send.at[off - 1, j],
            recv_sem=cross_recv.at[off - 1, j],
            device_id={"node": lax.rem(node + off, nodes)},
            device_id_type=MESH,
        )

    def piece_copy(peer, slot, cols):
        return pltpu.make_async_remote_copy(
            src_ref=piece_out.at[peer, :, cols],
            dst_ref=piece_in.at[slot, :, cols],
            send_sem=piece_send.at[peer],
            recv_sem=piece_recv.at[slot],
            device_id={"local": peer},
            device_id_type=MESH,
        )

    def project_down(j):
        for copy in down_copies(j):
            copy.wait()
        total = jnp.dot(act[:, :chunk], slots[j, :, :chunk], preferred_element_type=jnp.float32)
        for b in range(1, blocks):
            span = slice(b * chunk, (b + 1) * chunk)
            total += jnp.dot(act[:, span], slots[j, :, span], preferred_element_type=jnp.float32)
        for group in range(nodes):
            weighted[j, group] = total[group * half : (group + 1) * half]
        for off in range(1, nodes):
            cross_out[off - 1, j] = weighted[j, lax.rem(node + off, nodes)].astype(jnp.bfloat16)
            cross_copy(off, j).start()

    def send_pieces(j):
        total = weighted[j, node]
        for off in range(1, nodes):
            cross_copy(off, j).wait_recv()
            total += cross_in[off - 1, j].astype(jnp.float32)
        cols = chunk_cols(j)
        for peer in range(locals_):
            piece_out[peer, :, cols] = total[peer * toks : (peer + 1) * toks].astype(jnp.bfloat16)
        peer_loop(1, lambda peer: piece_copy(peer, local, cols).start())

    project_down(0)

    def down_step(j, carry):
        project_down(j)
        send_pieces(j - 1)
        return carry

    lax.fori_loop(1, pairs, down_step, 0)
    send_pieces(pairs - 1)
    piece_in[local] = piece_out[local]
    peer_loop(1, lambda peer: piece_copy(peer, peer, every).wait_recv())
    for s in range(stages):
        cols = stage_cols(s)
        summed = hidden[:, cols]
        for peer in range(locals_):
            summed += piece_in[peer, :, cols].astype(jnp.float32)
        out_ref[:, cols] = summed.astype(jnp.bfloat16)

    def drain(peer):
        part_copy(peer, local, None).wait_send()
        gather_copy(peer, me, None).wait_send()
        meta_copy(peer, me).wait_send()
        piece_copy(peer, local, every).wait_send()

    peer_loop(1, drain)

    def drain_relay(peer):
        for off in range(1, nodes):
            relay_copy(off, node * locals_ + peer, None).wait_send()
            meta_relay(off, node * locals_ + peer).wait_send()

    peer_loop(0, drain_relay)

    def drain_cross(j, carry):
        for off in range(1, nodes):
            cross_copy(off, j).wait_send()
        return carry

    lax.fori_loop(0, pairs, drain_cross, 0)


def solution(mesh):
    nodes, locals_ = mesh.shape["node"], mesh.shape["local"]
    members = nodes * locals_

    def shards(attn_out, o_proj, resid, norm_gain, routes, route_w, w_gate, w_up, w_down):
        toks, width = resid.shape
        hidden_units = w_gate.shape[2]
        chunk = next(c for c in (512, 256, 128) if hidden_units % c == 0 and width % c == 0)
        pairs = width // chunk
        blocks = hidden_units // chunk
        stages = next(n for n in (7, 4, 2, 1) if pairs % n == 0)
        bf16, f32 = jnp.bfloat16, jnp.float32
        vmem = pl.BlockSpec(memory_space=pltpu.VMEM)
        hbm = pl.BlockSpec(memory_space=pl.ANY)
        dma = pltpu.SemaphoreType.DMA
        total = members * toks
        return pl.pallas_call(
            functools.partial(layer_kernel, nodes, locals_, stages),
            out_shape=jax.ShapeDtypeStruct((toks, width), bf16),
            in_specs=[vmem, hbm, vmem, vmem, vmem, vmem, hbm, hbm, hbm],
            out_specs=vmem,
            scratch_shapes=[
                pltpu.VMEM(o_proj.shape, bf16),
                pltpu.VMEM((2 * pairs, chunk, hidden_units), bf16),
                pltpu.VMEM((locals_, toks, width), bf16),
                pltpu.VMEM((locals_, toks, width), bf16),
                pltpu.VMEM((toks, width), f32),
                pltpu.VMEM((members, toks, width), bf16),
                pltpu.VMEM((total, width), bf16),
                pltpu.VMEM((members, toks, 128), f32),
                pltpu.VMEM((total, 128), f32),
                pltpu.VMEM((total, hidden_units), f32),
                pltpu.VMEM((total, hidden_units), f32),
                pltpu.VMEM((total, hidden_units), bf16),
                pltpu.VMEM((pairs, nodes, locals_ * toks, chunk), f32),
                pltpu.VMEM((nodes - 1, pairs, locals_ * toks, chunk), bf16),
                pltpu.VMEM((nodes - 1, pairs, locals_ * toks, chunk), bf16),
                pltpu.VMEM((locals_, toks, width), bf16),
                pltpu.VMEM((locals_, toks, width), bf16),
                dma,
                dma((2 * pairs, blocks)),
                dma((locals_,)),
                dma((locals_, stages)),
                dma((locals_,)),
                dma((members, stages)),
                dma((nodes - 1, locals_)),
                dma((locals_,)),
                dma((members,)),
                dma((nodes - 1, locals_)),
                dma((nodes - 1, pairs)),
                dma((nodes - 1, pairs)),
                dma((locals_,)),
                dma((locals_,)),
            ],
            compiler_params=pltpu.CompilerParams(
                collective_id=0, has_side_effects=True, vmem_limit_bytes=67043328
            ),
            name="moe_layer",
        )(attn_out, o_proj, resid, norm_gain.reshape(1, width), routes, route_w, w_gate, w_up, w_down)

    placed = (
        P(("rep", "node"), "local"),
        P("local", None),
        P(("rep", "node", "local"), None),
        P(),
        P(("rep", "node", "local"), None),
        P(("rep", "node", "local"), None),
        P(("node", "local"), None, None),
        P(("node", "local"), None, None),
        P(("node", "local"), None, None),
    )
    return jax.shard_map(
        shards,
        mesh=mesh,
        in_specs=placed,
        out_specs=P(("rep", "node", "local"), None),
        check_vma=False,
    )
```

```python
import functools

import jax
import jax.numpy as jnp
from jax import lax
from jax.experimental import pallas as pl
from jax.experimental.pallas import tpu as pltpu
from jax.sharding import PartitionSpec as P

GROUP_EXPERTS = 8
MESH = pl.DeviceIdType.MESH


def layer_kernel(
    nodes,
    locals_,
    stages,
    attn_ref,
    oproj_hbm,
    resid_ref,
    gain_ref,
    routes_ref,
    weight_ref,
    gate_hbm,
    up_hbm,
    down_hbm,
    out_ref,
    oproj,
    slots,
    part_out,
    part_in,
    hidden,
    gathered,
    rows,
    meta,
    meta_rows,
    gate_acc,
    up_acc,
    act,
    weighted,
    cross_out,
    cross_in,
    piece_out,
    piece_in,
    oproj_sem,
    slot_sem,
    part_send,
    part_recv,
    gather_send,
    gather_recv,
    relay_send,
    meta_send,
    meta_recv,
    meta_relay_send,
    cross_send,
    cross_recv,
    piece_send,
    piece_recv,
):
    node = lax.axis_index("node")
    local = lax.axis_index("local")
    members = nodes * locals_
    me = node * locals_ + local
    chunk, hidden_units = slots.shape[1], slots.shape[2]
    blocks = hidden_units // chunk
    toks, width = resid_ref.shape
    pairs = width // chunk
    stage_width = width // stages
    stage_pairs = pairs // stages
    half = locals_ * toks
    group_chunks = 2 if pairs % 2 == 0 else 1
    lag = min(3, pairs)
    every = pl.ds(0, width)

    def stage_cols(s):
        return every if s is None else pl.ds(s * stage_width, stage_width)

    def chunk_cols(j):
        return pl.ds(pl.multiple_of(j * chunk, chunk), chunk)

    def peer_loop(first, body):
        def step(dist, carry):
            body(lax.rem(local + dist, locals_))
            return carry

        lax.fori_loop(first, locals_, step, 0)

    def up_copies(i):
        return (
            pltpu.make_async_copy(gate_hbm.at[0, chunk_cols(i)], slots.at[2 * i], slot_sem.at[2 * i, 0]),
            pltpu.make_async_copy(up_hbm.at[0, chunk_cols(i)], slots.at[2 * i + 1], slot_sem.at[2 * i + 1, 0]),
        )

    def down_copies(j):
        return [
            pltpu.make_async_copy(
                down_hbm.at[0, pl.ds(b * chunk, chunk), chunk_cols(j)],
                slots.at[j, :, pl.ds(b * chunk, chunk)],
                slot_sem.at[j, b],
            )
            for b in range(blocks)
        ]

    load_oproj = pltpu.make_async_copy(oproj_hbm, oproj, oproj_sem)
    load_oproj.start()

    barrier = pltpu.get_barrier_semaphore()

    def greet(peer):
        pl.semaphore_signal(barrier, inc=1, device_id={"local": peer}, device_id_type=MESH)

    peer_loop(1, greet)
    for off in range(1, nodes):
        pl.semaphore_signal(
            barrier, inc=1, device_id={"node": lax.rem(node + off, nodes)}, device_id_type=MESH
        )

    def fill(i, carry):
        for copy in up_copies(i):
            copy.start()
        return carry

    lax.fori_loop(0, pairs, fill, 0)

    def part_copy(peer, slot, s):
        return pltpu.make_async_remote_copy(
            src_ref=part_out.at[peer, :, stage_cols(s)],
            dst_ref=part_in.at[slot, :, stage_cols(s)],
            send_sem=part_send.at[peer],
            recv_sem=part_recv.at[slot, s or 0],
            device_id={"local": peer},
            device_id_type=MESH,
        )

    def gather_copy(peer, slot, s):
        return pltpu.make_async_remote_copy(
            src_ref=gathered.at[slot, :, stage_cols(s)],
            dst_ref=gathered.at[slot, :, stage_cols(s)],
            send_sem=gather_send.at[peer],
            recv_sem=gather_recv.at[slot, s or 0],
            device_id={"local": peer},
            device_id_type=MESH,
        )

    def relay_copy(off, slot, s):
        return pltpu.make_async_remote_copy(
            src_ref=gathered.at[slot, :, stage_cols(s)],
            dst_ref=gathered.at[slot, :, stage_cols(s)],
            send_sem=relay_send.at[off - 1, lax.rem(slot, locals_)],
            recv_sem=gather_recv.at[slot, s or 0],
            device_id={"node": lax.rem(node + off, nodes)},
            device_id_type=MESH,
        )

    def meta_copy(peer, slot):
        return pltpu.make_async_remote_copy(
            src_ref=meta.at[slot],
            dst_ref=meta.at[slot],
            send_sem=meta_send.at[peer],
            recv_sem=meta_recv.at[slot],
            device_id={"local": peer},
            device_id_type=MESH,
        )

    def meta_relay(off, slot):
        return pltpu.make_async_remote_copy(
            src_ref=meta.at[slot],
            dst_ref=meta.at[slot],
            send_sem=meta_relay_send.at[off - 1, lax.rem(slot, locals_)],
            recv_sem=meta_recv.at[slot],
            device_id={"node": lax.rem(node + off, nodes)},
            device_id_type=MESH,
        )

    load_oproj.wait()
    for s in range(stages):
        cols = stage_cols(s)
        partial = jnp.dot(attn_ref[...], oproj[:, cols], preferred_element_type=jnp.float32)
        for peer in range(locals_):
            part_out[peer, :, cols] = partial[peer * toks : (peer + 1) * toks].astype(jnp.bfloat16)
        if s == 0:
            pl.semaphore_wait(barrier, locals_ - 1 + nodes - 1)
        peer_loop(1, lambda peer: part_copy(peer, local, s).start())

    gate_acc[...] = jnp.zeros_like(gate_acc)
    up_acc[...] = jnp.zeros_like(up_acc)

    def reduce_stage(s):
        cols = stage_cols(s)
        peer_loop(1, lambda peer: part_copy(peer, peer, s).wait_recv())
        part_in[local, :, cols] = part_out[local, :, cols]
        value = resid_ref[:, cols].astype(jnp.float32)
        for peer in range(locals_):
            value += part_in[peer, :, cols].astype(jnp.float32)
        hidden[:, cols] = value
        gathered[me, :, cols] = (value * gain_ref[:, cols]).astype(jnp.bfloat16)
        peer_loop(1, lambda peer: gather_copy(peer, me, s).start())
        for off in range(1, nodes):
            relay_copy(off, me, s).start()

    def send_meta():
        value = hidden[...]
        scale = lax.rsqrt(jnp.mean(value * value, axis=-1, keepdims=True) + 1e-06)
        lane = lax.broadcasted_iota(jnp.int32, (toks, 128), 1)
        picks, scales = routes_ref[...], weight_ref[...].astype(jnp.float32)
        shares = jnp.zeros((toks, 128), jnp.float32)
        for k in range(picks.shape[1]):
            shares += jnp.where(picks[:, k : k + 1] == lane, scales[:, k : k + 1], 0.0)
        meta[me] = jnp.where(lane == 127, scale, shares)
        peer_loop(1, lambda peer: meta_copy(peer, me).start())
        for off in range(1, nodes):
            meta_relay(off, me).start()

    def relay_stage(s):
        def forward(peer):
            slot = node * locals_ + peer
            gather_copy(peer, slot, s).wait_recv()
            for off in range(1, nodes):
                relay_copy(off, slot, s).start()

        peer_loop(1, forward)

    def project_up(i, carry):
        for copy in up_copies(i):
            copy.wait()
        lhs = rows[:, chunk_cols(i)]
        gate_acc[...] += jnp.dot(lhs, slots[2 * i], preferred_element_type=jnp.float32)
        up_acc[...] += jnp.dot(lhs, slots[2 * i + 1], preferred_element_type=jnp.float32)
        for late in range(2):

            @pl.when(2 * i + late < pairs)
            def _():
                for copy in down_copies(2 * i + late):
                    copy.start()

        return carry

    def multiply_stage(s):
        def arrive(peer):
            for off in range(1, nodes):
                relay_copy(off, lax.rem(node + off, nodes) * locals_ + peer, s).wait_recv()

        peer_loop(0, arrive)
        cols = stage_cols(s)
        for member in range(members):
            rows[member * toks : (member + 1) * toks, cols] = gathered[member, :, cols]
        lax.fori_loop(s * stage_pairs, (s + 1) * stage_pairs, project_up, 0)

    for step in range(stages + 2):
        if step < stages:
            reduce_stage(step)
        if step == stages - 1:
            send_meta()
        if 1 <= step <= stages:
            relay_stage(step - 1)
        if step == stages:

            def forward_meta(peer):
                slot = node * locals_ + peer
                meta_copy(peer, slot).wait_recv()
                for off in range(1, nodes):
                    meta_relay(off, slot).start()

            peer_loop(1, forward_meta)
        if step >= 2:
            multiply_stage(step - 2)

    def meta_arrive(peer):
        for off in range(1, nodes):
            meta_relay(off, lax.rem(node + off, nodes) * locals_ + peer).wait_recv()

    peer_loop(0, meta_arrive)
    for member in range(members):
        meta_rows[member * toks : (member + 1) * toks, :] = meta[member]
    facts = meta_rows[...]
    lane = lax.broadcasted_iota(jnp.int32, facts.shape, 1)
    expert = lax.div(me, locals_ // GROUP_EXPERTS)
    share = jnp.sum(jnp.where(lane == expert, facts, 0.0), axis=1, keepdims=True)
    scale = jnp.sum(jnp.where(lane == 127, facts, 0.0), axis=1, keepdims=True)
    for b in range(blocks):
        span = slice(b * chunk, (b + 1) * chunk)
        gate_val = gate_acc[:, span] * scale
        up_val = up_acc[:, span] * (scale * share)
        act[:, span] = (gate_val / (1.0 + jnp.exp(-gate_val)) * up_val).astype(jnp.bfloat16)

    def cross_copy(off, j):
        return pltpu.make_async_remote_copy(
            src_ref=cross_out.at[off - 1, j],
            dst_ref=cross_in.at[off - 1, j],
            send_sem=cross_send.at[off - 1, j],
            recv_sem=cross_recv.at[off - 1, j],
            device_id={"node": lax.rem(node + off, nodes)},
            device_id_type=MESH,
        )

    def piece_copy(peer, slot, cols):
        return pltpu.make_async_remote_copy(
            src_ref=piece_out.at[peer, :, cols],
            dst_ref=piece_in.at[slot, :, cols],
            send_sem=piece_send.at[peer],
            recv_sem=piece_recv.at[slot],
            device_id={"local": peer},
            device_id_type=MESH,
        )

    def project_down(j):
        for copy in down_copies(j):
            copy.wait()
        total = jnp.dot(act[:, :chunk], slots[j, :, :chunk], preferred_element_type=jnp.float32)
        for b in range(1, blocks):
            span = slice(b * chunk, (b + 1) * chunk)
            total += jnp.dot(act[:, span], slots[j, :, span], preferred_element_type=jnp.float32)
        for group in range(nodes):
            weighted[j, group] = total[group * half : (group + 1) * half]
        for off in range(1, nodes):
            cross_out[off - 1, j] = weighted[j, lax.rem(node + off, nodes)].astype(jnp.bfloat16)
            cross_copy(off, j).start()

    def send_pieces(j):
        total = weighted[j, node]
        for off in range(1, nodes):
            cross_copy(off, j).wait_recv()
            total += cross_in[off - 1, j].astype(jnp.float32)
        cols = chunk_cols(j)
        for peer in range(locals_):
            piece_out[peer, :, cols] = total[peer * toks : (peer + 1) * toks].astype(jnp.bfloat16)

        @pl.when(j % group_chunks == group_chunks - 1)
        def _():
            first = pl.multiple_of((j - group_chunks + 1) * chunk, chunk)
            sent = pl.ds(first, group_chunks * chunk)
            peer_loop(1, lambda peer: piece_copy(peer, local, sent).start())

    def down_start(j, carry):
        project_down(j)
        return carry

    def down_step(j, carry):
        project_down(j)
        send_pieces(j - lag)
        return carry

    def down_finish(j, carry):
        send_pieces(j)
        return carry

    lax.fori_loop(0, lag, down_start, 0)
    lax.fori_loop(lag, pairs, down_step, 0)
    lax.fori_loop(pairs - lag, pairs, down_finish, 0)
    piece_in[local] = piece_out[local]
    peer_loop(1, lambda peer: piece_copy(peer, peer, every).wait_recv())
    for s in range(stages):
        cols = stage_cols(s)
        summed = hidden[:, cols]
        for peer in range(locals_):
            summed += piece_in[peer, :, cols].astype(jnp.float32)
        out_ref[:, cols] = summed.astype(jnp.bfloat16)

    def drain(peer):
        part_copy(peer, local, None).wait_send()
        gather_copy(peer, me, None).wait_send()
        meta_copy(peer, me).wait_send()
        piece_copy(peer, local, every).wait_send()

    peer_loop(1, drain)

    def drain_relay(peer):
        for off in range(1, nodes):
            relay_copy(off, node * locals_ + peer, None).wait_send()
            meta_relay(off, node * locals_ + peer).wait_send()

    peer_loop(0, drain_relay)

    def drain_cross(j, carry):
        for off in range(1, nodes):
            cross_copy(off, j).wait_send()
        return carry

    lax.fori_loop(0, pairs, drain_cross, 0)


def solution(mesh):
    nodes, locals_ = mesh.shape["node"], mesh.shape["local"]
    members = nodes * locals_

    def shards(attn_out, o_proj, resid, norm_gain, routes, route_w, w_gate, w_up, w_down):
        toks, width = resid.shape
        hidden_units = w_gate.shape[2]
        chunk = next(c for c in (512, 256, 128) if hidden_units % c == 0 and width % c == 0)
        pairs = width // chunk
        blocks = hidden_units // chunk
        stages = next(n for n in (2, 1) if pairs % n == 0)
        bf16, f32 = jnp.bfloat16, jnp.float32
        vmem = pl.BlockSpec(memory_space=pltpu.VMEM)
        hbm = pl.BlockSpec(memory_space=pl.ANY)
        dma = pltpu.SemaphoreType.DMA
        total = members * toks
        return pl.pallas_call(
            functools.partial(layer_kernel, nodes, locals_, stages),
            out_shape=jax.ShapeDtypeStruct((toks, width), bf16),
            in_specs=[vmem, hbm, vmem, vmem, vmem, vmem, hbm, hbm, hbm],
            out_specs=vmem,
            scratch_shapes=[
                pltpu.VMEM(o_proj.shape, bf16),
                pltpu.VMEM((2 * pairs, chunk, hidden_units), bf16),
                pltpu.VMEM((locals_, toks, width), bf16),
                pltpu.VMEM((locals_, toks, width), bf16),
                pltpu.VMEM((toks, width), f32),
                pltpu.VMEM((members, toks, width), bf16),
                pltpu.VMEM((total, width), bf16),
                pltpu.VMEM((members, toks, 128), f32),
                pltpu.VMEM((total, 128), f32),
                pltpu.VMEM((total, hidden_units), f32),
                pltpu.VMEM((total, hidden_units), f32),
                pltpu.VMEM((total, hidden_units), bf16),
                pltpu.VMEM((pairs, nodes, locals_ * toks, chunk), f32),
                pltpu.VMEM((nodes - 1, pairs, locals_ * toks, chunk), bf16),
                pltpu.VMEM((nodes - 1, pairs, locals_ * toks, chunk), bf16),
                pltpu.VMEM((locals_, toks, width), bf16),
                pltpu.VMEM((locals_, toks, width), bf16),
                dma,
                dma((2 * pairs, blocks)),
                dma((locals_,)),
                dma((locals_, stages)),
                dma((locals_,)),
                dma((members, stages)),
                dma((nodes - 1, locals_)),
                dma((locals_,)),
                dma((members,)),
                dma((nodes - 1, locals_)),
                dma((nodes - 1, pairs)),
                dma((nodes - 1, pairs)),
                dma((locals_,)),
                dma((locals_,)),
            ],
            compiler_params=pltpu.CompilerParams(
                collective_id=0, has_side_effects=True, vmem_limit_bytes=67043328
            ),
            name="moe_layer",
        )(attn_out, o_proj, resid, norm_gain.reshape(1, width), routes, route_w, w_gate, w_up, w_down)

    placed = (
        P(("rep", "node"), "local"),
        P("local", None),
        P(("rep", "node", "local"), None),
        P(),
        P(("rep", "node", "local"), None),
        P(("rep", "node", "local"), None),
        P(("node", "local"), None, None),
        P(("node", "local"), None, None),
        P(("node", "local"), None, None),
    )
    return jax.shard_map(
        shards,
        mesh=mesh,
        in_specs=placed,
        out_specs=P(("rep", "node", "local"), None),
        check_vma=False,
    )
```
